256 devices in a mesh: row: 32 (over y, z_hi, core), col: 8 (over x, z_lo).
Axes of the slice: x: 4, y: 4, z: 8 (z_hi: 4, z_lo: 2; z = z_hi * 2 + z_lo), core: 2. Of those that a mesh axis runs over, the one named last changes fastest.
Arguments:
- activation: bfloat16 [2048, 2048, 128], P('row', 'col'), may hold values from -6 to 6
- kernel_one: bfloat16 [3, 3, 128, 128], replicated, may hold values from -0.1875 to 0.1875
- bias_one: float32 [128], replicated, may hold values from -0.5 to 0.5
- kernel_two: bfloat16 [3, 3, 128, 128], replicated, may hold values from -0.1875 to 0.1875
- bias_two: float32 [128], replicated, may hold values from -0.5 to 0.5
Outputs:
- result_map: bfloat16 [2048, 2048, 128], P('row', 'col')
The draws below stay inside these ranges and needn't reach their ends.
All inputs are finite; a program needn't handle non-finite values.
Results may differ from the reference program's by a relative error of at most 0.0095.
Values may be sent and summed in bfloat16 or wider, within the bound.
A program may use at most 64 MiB of HBM per device.

```python
import jax
import jax.numpy as jnp
from jax import lax

CH = 128
BLOCK = 64
NMAP = 2048
N_ROW = 32


def steps_of(rng, shape, shards, low, largest):
    loudness, own = 1.0, jax.random.fold_in(rng, 6)
    for axis_at, parts in shards:
        heights = jnp.exp(jax.random.uniform(jax.random.fold_in(own, axis_at), (parts,), jnp.float32, low / len(shards), largest / len(shards)))
        loudness = loudness * jnp.repeat(heights, shape[axis_at] // parts).reshape([-1 if axis == axis_at else 1 for axis in range(len(shape))])
    return loudness


def noise(key, extent, spread, limit, cuts=(), kind=jnp.bfloat16):
    array = jax.random.normal(key, extent, jnp.float32) * spread
    if len(cuts) > 0:
        array = steps_of(key, extent, cuts, -0.22, 0.18) * array
    return jnp.clip(array, min=-limit, max=limit).astype(kind)


def setup_inputs(seed: int = 0) -> dict:
    seeds = jax.random.split(jax.random.key(seed), 6)
    activation = noise(seeds[0], (NMAP, NMAP, CH), 1.0, 6.0, ((0, 32), (1, 8)))
    kernel_one = noise(seeds[1], (3, 3, CH, CH), (9 * CH) ** -0.5, 0.1875)
    bias_one = jnp.clip(jax.random.uniform(seeds[2], (CH,), jnp.float32, -0.5, 0.5), -0.5, 0.5)
    kernel_two = noise(seeds[3], (3, 3, CH, CH), (9 * CH) ** -0.5, 0.1875)
    bias_two = jnp.clip(jax.random.uniform(seeds[4], (CH,), jnp.float32, -0.5, 0.5), -0.5, 0.5)
    return {"activation": activation, "kernel_one": kernel_one, "bias_one": bias_one, "kernel_two": kernel_two, "bias_two": bias_two}


def convolve(padded_map, kernel, offset, start):
    band = lax.dynamic_slice_in_dim(padded_map, start, BLOCK + 8, 0).astype(jnp.float32)
    result = lax.conv_general_dilated(band[None], kernel.astype(jnp.float32), (1, 1), "VALID", rhs_dilation=(4, 4), dimension_numbers=("NHWC", "HWIO", "NHWC"), precision=lax.Precision.HIGHEST)[0]
    return result + offset


def reference(activation, kernel_one, bias_one, kernel_two, bias_two):
    padded_in = jnp.pad(activation, ((4, 4), (4, 4), (0, 0)))
    starts = jnp.arange(N_ROW, dtype=jnp.int32) * BLOCK

    def first_layer(start):
        return jax.nn.elu(convolve(padded_in, kernel_one, bias_one, start)).astype(jnp.bfloat16)

    elu_out = lax.map(first_layer, starts).reshape(NMAP, NMAP, CH)
    symmetric = (0.5 * (elu_out.astype(jnp.float32) + jnp.swapaxes(elu_out, 0, 1).astype(jnp.float32))).astype(jnp.bfloat16)
    padded_sym = jnp.pad(symmetric, ((4, 4), (4, 4), (0, 0)))

    def second_layer(start):
        resid = lax.dynamic_slice_in_dim(symmetric, start, BLOCK, 0).astype(jnp.float32)
        return (resid + convolve(padded_sym, kernel_two, bias_two, start)).astype(jnp.bfloat16)

    return lax.map(second_layer, starts).reshape(NMAP, NMAP, CH)
```

```python
import functools

import jax
import jax.numpy as jnp
from jax import lax
from jax.experimental import pallas as pl
from jax.experimental.pallas import tpu as pltpu
from jax.sharding import PartitionSpec as P

MESH = pl.DeviceIdType.MESH
F32, BF16 = jnp.float32, jnp.bfloat16
SLABS = 8
SIDES = ((-1, 0), (1, 0), (0, -1), (0, 1), (-1, -1), (-1, 1), (1, -1), (1, 1))


def select(rule, value):
    row = lax.broadcasted_iota(jnp.int32, (256, 256), 0)
    col = lax.broadcasted_iota(jnp.int32, (256, 256), 1)
    return jnp.where(rule(row) == col, value, 0.0).astype(BF16)


def to_phase(i):
    return ((i >> 2) & 3) * 64 + (i >> 4) * 4 + (i & 3)


def from_phase(i):
    return ((i >> 2) & 15) * 16 + (i >> 6) * 4 + (i & 3)


def swap_phase(i):
    return (i & ~15) + (i & 3) * 4 + ((i >> 2) & 3)


def taps(padded, line, first, count, weight):
    parts = [
        padded[line + u, pl.ds(first + w, count)].reshape(count * 16, 128)
        for u in range(3)
        for w in range(3)
    ]
    return jnp.dot(jnp.concatenate(parts, axis=1), weight[...], preferred_element_type=F32)


def kernel(
    x_hbm, k1, b1, k2, b2, out_hbm,
    flat, xpad, e, m, relay, spad, p_in, p_swap, p_out,
    in_sem, out_sem, halo_send, halo_recv, e_sem, f_sem, m_sem, r_sem,
):
    r, c = lax.axis_index("row"), lax.axis_index("col")
    y, x, core = r // 8, c // 2, r % 2
    z2, z1, z0 = (r // 4) % 2, (r // 2) % 2, c % 2
    mine = 2 * z1 + core
    diag = x == y
    slot = jnp.maximum((y - x + 4) % 4 - 1, 0)

    def load(s):
        rows = pl.ds(16 * s, 16)
        return pltpu.make_async_copy(x_hbm.at[rows], flat.at[rows], in_sem.at[s])

    def save(line):
        rows = pl.ds(4 * line, 4)
        return pltpu.make_async_copy(flat.at[rows], out_hbm.at[rows], out_sem.at[line])

    def there(dr, dc):
        return (r + dr >= 0) & (r + dr < 32) & (c + dc >= 0) & (c + dc < 8)

    def edge(buf, which, n):
        dr, dc = SIDES[n]
        near = lambda d, last: pl.ds(1, last) if d == 0 else pl.ds(1 if d < 0 else last, 1)
        far = lambda d, last: pl.ds(1, last) if d == 0 else pl.ds(last + 1 if d < 0 else 0, 1)
        return pltpu.make_async_remote_copy(
            buf.at[near(dr, 16), near(dc, 64)],
            buf.at[far(dr, 16), far(dc, 64)],
            halo_send.at[which, n],
            halo_recv.at[which, n],
            device_id=(r + dr, c + dc),
            device_id_type=MESH,
        )

    def clear(buf):
        zero_row = jnp.zeros((66, 16, 128), BF16)
        zero_col = jnp.zeros((18, 16, 128), BF16)
        for cond, line in ((r == 0, 0), (r == 31, 17)):
            @pl.when(cond)
            def _():
                buf[line] = zero_row
        for cond, line in ((c == 0, 0), (c == 7, 65)):
            @pl.when(cond)
            def _():
                buf[:, line] = zero_col

    def halo_start(buf, which):
        for n, side in enumerate(SIDES):
            @pl.when(there(*side))
            def _():
                edge(buf, which, n).start()

    def halo_wait(buf, which):
        for n, (dr, dc) in enumerate(SIDES):
            back = SIDES.index((-dr, -dc))

            @pl.when(there(dr, dc))
            def _():
                edge(buf, which, n).wait_send()
                edge(buf, which, back).wait_recv()

    def owner(to_y, to_x, k):
        return (to_y * 8 + 4 * z0 + k, to_x * 2 + z2)

    def block(q, t, k):
        return e.at[2 * q + t, pl.ds(16 * k, 16)]

    def push(q, t, k, dst, sem, device):
        return pltpu.make_async_remote_copy(
            block(q, t, k), dst, e_sem.at[q, t, k], sem, device_id=device, device_id_type=MESH
        )

    def final(k):
        to = owner(x, y, k)
        return to, (to[0] == r) & (to[1] == c)

    def send(q):
        for t in range(2):
            for kk in range(4):
                k = (kk + mine) % 4
                to, here = final(k)
                dst, sem = m.at[2 * q + t, mine], m_sem.at[q, t, mine]
                direct = jnp.logical_not(here)

                @pl.when(direct if t == 0 else direct & diag)
                def _():
                    push(q, t, k, dst, sem, to).start()

                @pl.when(here)
                def _():
                    dst[...] = block(q, t, k)[...]

                if t == 1:
                    @pl.when(jnp.logical_not(diag))
                    def _():
                        push(q, t, k, relay.at[slot, q, mine], r_sem.at[slot, q, mine], owner(x, x, k)).start()

    def forward(q, i):
        return pltpu.make_async_remote_copy(
            relay.at[i, q],
            m.at[2 * q + 1],
            f_sem.at[i, q],
            m_sem.at[q, 1, 0],
            device_id=(r, ((x + 1 + i) % 4) * 2 + z0),
            device_id_type=MESH,
        )

    def received(q, t, j):
        return push(q, t, j, m.at[2 * q + t, j], m_sem.at[q, t, j], (r, c))

    def arrive(q, t, j):
        _, here = final(j)

        @pl.when(jnp.logical_not(here))
        def _():
            received(q, t, j).wait_recv()

    for s in range(4):
        load(s).start()
    p_in[...] = select(to_phase, 1.0)
    p_swap[...] = select(swap_phase, 0.5)
    p_out[...] = select(from_phase, 1.0)
    clear(xpad)
    clear(spad)
    for s in range(4):
        load(s).wait()

        @pl.loop(4 * s, 4 * s + 4)
        def _(line):
            for g in range(4):
                rows = flat[pl.ds(4 * line, 4), pl.ds(64 * g, 64)].reshape(256, 128)
                moved = jnp.dot(p_in[...], rows, preferred_element_type=F32).astype(BF16)
                xpad[line + 1, pl.ds(1 + 16 * g, 16)] = moved.reshape(16, 16, 128)

    halo_start(xpad, 0)
    halo_wait(xpad, 0)

    @pl.loop(0, SLABS)
    def _(q):
        for t in range(2):
            for g in range(2):
                v = taps(xpad, 2 * q + t, 32 * g, 32, k1) + b1[...]
                v = jnp.where(v > 0, v, jnp.exp(jnp.minimum(v, 0.0)) - 1.0)
                e[2 * q + t, pl.ds(32 * g, 32)] = v.astype(BF16).reshape(32, 16, 128)
        send(q)

    @pl.loop(0, SLABS)
    def _(q):
        @pl.when(diag)
        def _():
            for i in range(3):
                for j in range(4):
                    pltpu.make_async_remote_copy(
                        block(q, 1, j), relay.at[i, q, j], e_sem.at[q, 1, j], r_sem.at[i, q, j],
                        device_id=(r, c), device_id_type=MESH,
                    ).wait_recv()
                forward(q, i).start()

    @pl.loop(0, SLABS)
    def _(q):
        for j in range(4):
            arrive(q, 0, j)

        @pl.when(diag)
        def _():
            for j in range(4):
                arrive(q, 1, j)

        @pl.when(jnp.logical_not(diag))
        def _():
            forward(q, 0).wait_recv()

        for t in range(2):
            for j in range(4):
                col = 16 * j + 2 * q + t
                moved = jnp.dot(p_swap[...], m[2 * q + t, j].reshape(256, 128), preferred_element_type=F32)
                own = e[:, col].reshape(256, 128).astype(F32)
                spad[pl.ds(1, 16), col + 1] = (0.5 * own + moved).astype(BF16).reshape(16, 16, 128)

    halo_start(spad, 1)
    halo_wait(spad, 1)

    @pl.loop(0, 16)
    def _(line):
        for g in range(2):
            v = taps(spad, line, 32 * g, 32, k2) + b2[...]
            v = v + spad[line + 1, pl.ds(1 + 32 * g, 32)].reshape(512, 128).astype(F32)
            v = v.astype(BF16)
            for h in range(2):
                moved = jnp.dot(p_out[...], v[256 * h : 256 * h + 256], preferred_element_type=F32)
                flat[pl.ds(4 * line, 4), pl.ds(128 * g + 64 * h, 64)] = moved.astype(BF16).reshape(4, 64, 128)
        save(line).start()

    @pl.loop(0, SLABS)
    def _(q):
        for t in range(2):
            for k in range(4):
                _, here = final(k)

                @pl.when(jnp.logical_not(here))
                def _():
                    received(q, t, k).wait_send()

        @pl.when(diag)
        def _():
            for i in range(3):
                forward(q, i).wait_send()

    @pl.loop(0, 16)
    def _(line):
        save(line).wait()


def body(activation, kernel_one, bias_one, kernel_two, bias_two):
    vmem, hbm = pl.BlockSpec(memory_space=pltpu.VMEM), pl.BlockSpec(memory_space=pl.ANY)
    dma = pltpu.SemaphoreType.DMA
    return pl.pallas_call(
        kernel,
        out_shape=jax.ShapeDtypeStruct(activation.shape, BF16),
        in_specs=[hbm, vmem, vmem, vmem, vmem],
        out_specs=hbm,
        scratch_shapes=[
            pltpu.VMEM((64, 256, 128), BF16),
            pltpu.VMEM((18, 66, 16, 128), BF16),
            pltpu.VMEM((16, 64, 16, 128), BF16),
            pltpu.VMEM((16, 4, 16, 16, 128), BF16),
            pltpu.VMEM((3, SLABS, 4, 16, 16, 128), BF16),
            pltpu.VMEM((18, 66, 16, 128), BF16),
            pltpu.VMEM((256, 256), BF16),
            pltpu.VMEM((256, 256), BF16),
            pltpu.VMEM((256, 256), BF16),
            dma((4,)),
            dma((16,)),
            dma((2, 8)),
            dma((2, 8)),
            dma((SLABS, 2, 4)),
            dma((3, SLABS)),
            dma((SLABS, 2, 4)),
            dma((3, SLABS, 4)),
        ],
        compiler_params=pltpu.CompilerParams(has_side_effects=True, vmem_limit_bytes=60 << 20),
        name="resblock",
    )(
        activation,
        kernel_one.reshape(1152, 128),
        bias_one.reshape(1, 128),
        kernel_two.reshape(1152, 128),
        bias_two.reshape(1, 128),
    )


def solution(mesh):
    in_specs = (P("row", "col", None), P(), P(), P(), P())
    out_specs = P("row", "col", None)
    return jax.shard_map(body, mesh=mesh, in_specs=in_specs, out_specs=out_specs, check_vma=False)
```

```python
import functools

import jax
import jax.numpy as jnp
from jax import lax
from jax.experimental import pallas as pl
from jax.experimental.pallas import tpu as pltpu
from jax.sharding import PartitionSpec as P

MESH = pl.DeviceIdType.MESH
F32, BF16 = jnp.float32, jnp.bfloat16
LINES = 16
LAG = 3
SIDES = ((-1, 0), (1, 0), (0, -1), (0, 1), (-1, -1), (-1, 1), (1, -1), (1, 1))


def select(rule, value):
    row = lax.broadcasted_iota(jnp.int32, (256, 256), 0)
    col = lax.broadcasted_iota(jnp.int32, (256, 256), 1)
    return jnp.where(rule(row) == col, value, 0.0).astype(BF16)


def to_phase(i):
    return ((i >> 2) & 3) * 64 + (i >> 4) * 4 + (i & 3)


def from_phase(i):
    return ((i >> 2) & 15) * 16 + (i >> 6) * 4 + (i & 3)


def swap_phase(i):
    return (i & ~15) + (i & 3) * 4 + ((i >> 2) & 3)


def taps(padded, line, first, count, weight):
    parts = [
        padded[line + u, pl.ds(first + w, count)].reshape(count * 16, 128)
        for u in range(3)
        for w in range(3)
    ]
    return jnp.dot(jnp.concatenate(parts, axis=1), weight[...], preferred_element_type=F32)


def kernel(
    x_hbm, k1, b1, k2, b2, out_hbm,
    flat, xpad, e, m, plane, cross, bridge, spad, p_in, p_swap, p_out,
    in_sem, out_sem, halo_send, halo_recv,
    plane_send, plane_recv, cross_send, cross_recv, e_sem, m_sem, bridge_send, bridge_recv,
):
    r, c = lax.axis_index("row"), lax.axis_index("col")
    y, x, core = r // 8, c // 2, r % 2
    z2, z1, z0 = (r // 4) % 2, (r // 2) % 2, c % 2
    z = 4 * z2 + 2 * z1 + z0
    mine = 2 * z1 + core
    apart = (y - x + 4) % 4
    diag, far = apart == 0, apart == 2
    near = (apart == 1) | (apart == 3)
    side = jnp.where(apart == 1, 0, 1)
    detour, bridging = (z == 3) | (z == 6), (z == 0) | (z == 1)

    def load(s):
        rows = pl.ds(16 * s, 16)
        return pltpu.make_async_copy(x_hbm.at[rows], flat.at[rows], in_sem.at[s])

    def save(line):
        rows = pl.ds(4 * line, 4)
        return pltpu.make_async_copy(flat.at[rows], out_hbm.at[rows], out_sem.at[line])

    def there(dr, dc):
        return (r + dr >= 0) & (r + dr < 32) & (c + dc >= 0) & (c + dc < 8)

    def edge(buf, which, n):
        dr, dc = SIDES[n]
        near = lambda d, last: pl.ds(1, last) if d == 0 else pl.ds(1 if d < 0 else last, 1)
        far = lambda d, last: pl.ds(1, last) if d == 0 else pl.ds(last + 1 if d < 0 else 0, 1)
        return pltpu.make_async_remote_copy(
            buf.at[near(dr, 16), near(dc, 64)],
            buf.at[far(dr, 16), far(dc, 64)],
            halo_send.at[which, n],
            halo_recv.at[which, n],
            device_id=(r + dr, c + dc),
            device_id_type=MESH,
        )

    def clear(buf):
        zero_row = jnp.zeros((66, 16, 128), BF16)
        zero_col = jnp.zeros((18, 16, 128), BF16)
        for cond, line in ((r == 0, 0), (r == 31, 17)):
            @pl.when(cond)
            def _():
                buf[line] = zero_row
        for cond, line in ((c == 0, 0), (c == 7, 65)):
            @pl.when(cond)
            def _():
                buf[:, line] = zero_col

    def halo_start(buf, which):
        for n, side in enumerate(SIDES):
            @pl.when(there(*side))
            def _():
                edge(buf, which, n).start()

    def halo_wait(buf, which):
        for n, (dr, dc) in enumerate(SIDES):
            back = SIDES.index((-dr, -dc))

            @pl.when(there(dr, dc))
            def _():
                edge(buf, which, n).wait_send()
                edge(buf, which, back).wait_recv()

    def copy(src, dst, send, recv, device):
        return pltpu.make_async_remote_copy(src, dst, send, recv, device_id=device, device_id_type=MESH)

    def chip(to_x, to_y):
        return (r - 8 * y + 8 * to_y, c - 2 * x + 2 * to_x)

    def to_mirror(line):
        return copy(e.at[line], plane.at[line], plane_send.at[line], plane_recv.at[line], chip(y, x))

    def to_corner(line):
        return copy(e.at[line], cross.at[side, line], plane_send.at[line], cross_recv.at[side, line], chip(x, x))

    def pass_on(line, n):
        to_x = (x + 1 + 2 * n) % 4
        return copy(cross.at[n, line], plane.at[line], cross_send.at[n, line], plane_recv.at[line], chip(to_x, y))

    def at_corner(line, n):
        return copy(cross.at[n, line], cross.at[n, line], cross_send.at[n, line], cross_recv.at[n, line], (r, c))

    def stays(k):
        return (z0 == z2) & (k == mine)

    def upright(src, line, k, dst, recv, device):
        return copy(src.at[line, pl.ds(16 * k, 16)], dst, e_sem.at[line, k], recv, device)

    def spread(line, src):
        for kk in range(4):
            k = (kk + mine) % 4
            around = detour & (k // 2 == 1) & (line % 2 == 0)
            half, low = line // 2, k % 2

            @pl.when(jnp.logical_not(stays(k)) & jnp.logical_not(around))
            def _():
                to = (8 * y + 4 * z0 + k, 2 * x + z2)
                upright(src, line, k, m.at[line, mine], m_sem.at[line, mine], to).start()

            @pl.when(stays(k))
            def _():
                m[line, mine] = src[line, pl.ds(16 * k, 16)]

            @pl.when(around)
            def _():
                to = (8 * y + core, 2 * x + jnp.where(z == 3, 0, 1))
                upright(src, line, k, bridge.at[half, low], bridge_recv.at[half, low], to).start()

    def bridge_on(half, low):
        to = (8 * y + jnp.where(z == 0, 6, 2) + low, 2 * x + jnp.where(z == 0, 0, 1))
        dst, recv = m.at[2 * half, 2 + core], m_sem.at[2 * half, 2 + core]
        return copy(bridge.at[half, low], dst, bridge_send.at[half, low], recv, to)

    def at_bridge(half, low):
        here = bridge.at[half, low]
        return copy(here, here, bridge_send.at[half, low], bridge_recv.at[half, low], (r, c))

    def route(line):
        @pl.when(diag)
        def _():
            for n in range(2):
                at_corner(line, n).wait_recv()
                pass_on(line, n).start()

        @pl.when(jnp.logical_not(diag))
        def _():
            to_mirror(line).wait_recv()
            spread(line, plane)

    def cross_over(line):
        @pl.when(bridging & (line % 2 == 0))
        def _():
            for low in range(2):
                at_bridge(line // 2, low).wait_recv()
                bridge_on(line // 2, low).start()

    def arrived(line, j):
        return upright(e, line, j, m.at[line, j], m_sem.at[line, j], (r, c))

    for s in range(4):
        load(s).start()
    p_in[...] = select(to_phase, 1.0)
    p_swap[...] = select(swap_phase, 0.5)
    p_out[...] = select(from_phase, 1.0)
    clear(xpad)
    clear(spad)
    for s in range(4):
        load(s).wait()

        @pl.loop(4 * s, 4 * s + 4)
        def _(line):
            for g in range(4):
                rows = flat[pl.ds(4 * line, 4), pl.ds(64 * g, 64)].reshape(256, 128)
                moved = jnp.dot(p_in[...], rows, preferred_element_type=F32).astype(BF16)
                xpad[line + 1, pl.ds(1 + 16 * g, 16)] = moved.reshape(16, 16, 128)

    halo_start(xpad, 0)
    halo_wait(xpad, 0)

    @pl.loop(0, LINES)
    def _(line):
        for g in range(2):
            v = taps(xpad, line, 32 * g, 32, k1) + b1[...]
            v = jnp.where(v > 0, v, jnp.exp(jnp.minimum(v, 0.0)) - 1.0)
            e[line, pl.ds(32 * g, 32)] = v.astype(BF16).reshape(32, 16, 128)

        @pl.when(near)
        def _():
            to_corner(line).start()

        @pl.when(far)
        def _():
            to_mirror(line).start()

        @pl.when(diag)
        def _():
            spread(line, e)

    @pl.loop(0, LAG)
    def _(line):
        route(line)

    @pl.loop(LAG, LINES)
    def _(line):
        route(line)
        cross_over(line - LAG)

    @pl.loop(LINES - LAG, LINES)
    def _(line):
        cross_over(line)

    @pl.loop(0, LINES)
    def _(line):
        for j in range(4):
            @pl.when(jnp.logical_not(stays(j)))
            def _():
                arrived(line, j).wait_recv()

        for j in range(4):
            col = 16 * j + line
            moved = jnp.dot(p_swap[...], m[line, j].reshape(256, 128), preferred_element_type=F32)
            own = e[:, col].reshape(256, 128).astype(F32)
            spad[pl.ds(1, 16), col + 1] = (0.5 * own + moved).astype(BF16).reshape(16, 16, 128)

    halo_start(spad, 1)
    halo_wait(spad, 1)

    @pl.loop(0, 16)
    def _(line):
        for g in range(2):
            v = taps(spad, line, 32 * g, 32, k2) + b2[...]
            v = v + spad[line + 1, pl.ds(1 + 32 * g, 32)].reshape(512, 128).astype(F32)
            v = v.astype(BF16)
            for h in range(2):
                moved = jnp.dot(p_out[...], v[256 * h : 256 * h + 256], preferred_element_type=F32)
                flat[pl.ds(4 * line, 4), pl.ds(128 * g + 64 * h, 64)] = moved.astype(BF16).reshape(4, 64, 128)
        save(line).start()

    @pl.loop(0, LINES)
    def _(line):
        for k in range(4):
            @pl.when(jnp.logical_not(stays(k)))
            def _():
                arrived(line, k).wait_send()

        @pl.when(diag)
        def _():
            for n in range(2):
                pass_on(line, n).wait_send()

        @pl.when(jnp.logical_not(diag))
        def _():
            to_mirror(line).wait_send()

        @pl.when(bridging & (line % 2 == 0))
        def _():
            for low in range(2):
                bridge_on(line // 2, low).wait_send()

    @pl.loop(0, 16)
    def _(line):
        save(line).wait()


def body(activation, kernel_one, bias_one, kernel_two, bias_two):
    vmem, hbm = pl.BlockSpec(memory_space=pltpu.VMEM), pl.BlockSpec(memory_space=pl.ANY)
    dma = pltpu.SemaphoreType.DMA
    return pl.pallas_call(
        kernel,
        out_shape=jax.ShapeDtypeStruct(activation.shape, BF16),
        in_specs=[hbm, vmem, vmem, vmem, vmem],
        out_specs=hbm,
        scratch_shapes=[
            pltpu.VMEM((64, 256, 128), BF16),
            pltpu.VMEM((18, 66, 16, 128), BF16),
            pltpu.VMEM((16, 64, 16, 128), BF16),
            pltpu.VMEM((16, 4, 16, 16, 128), BF16),
            pltpu.VMEM((16, 64, 16, 128), BF16),
            pltpu.VMEM((2, 16, 64, 16, 128), BF16),
            pltpu.VMEM((8, 2, 16, 16, 128), BF16),
            pltpu.VMEM((18, 66, 16, 128), BF16),
            pltpu.VMEM((256, 256), BF16),
            pltpu.VMEM((256, 256), BF16),
            pltpu.VMEM((256, 256), BF16),
            dma((4,)),
            dma((16,)),
            dma((2, 8)),
            dma((2, 8)),
            dma((16,)),
            dma((16,)),
            dma((2, 16)),
            dma((2, 16)),
            dma((16, 4)),
            dma((16, 4)),
            dma((8, 2)),
            dma((8, 2)),
        ],
        compiler_params=pltpu.CompilerParams(has_side_effects=True, vmem_limit_bytes=60 << 20),
        name="resblock",
    )(
        activation,
        kernel_one.reshape(1152, 128),
        bias_one.reshape(1, 128),
        kernel_two.reshape(1152, 128),
        bias_two.reshape(1, 128),
    )


def solution(mesh):
    in_specs = (P("row", "col", None), P(), P(), P(), P())
    out_specs = P("row", "col", None)
    return jax.shard_map(body, mesh=mesh, in_specs=in_specs, out_specs=out_specs, check_vma=False)
```

```python
import functools

import jax
import jax.numpy as jnp
from jax import lax
from jax.experimental import pallas as pl
from jax.experimental.pallas import tpu as pltpu
from jax.sharding import PartitionSpec as P

MESH = pl.DeviceIdType.MESH
F32, BF16 = jnp.float32, jnp.bfloat16
LINES = 16
LAG = 3
ROUTE = 8
SIDES = ((-1, 0), (1, 0), (0, -1), (0, 1), (-1, -1), (-1, 1), (1, -1), (1, 1))


def select(rule, value):
    row = lax.broadcasted_iota(jnp.int32, (256, 256), 0)
    col = lax.broadcasted_iota(jnp.int32, (256, 256), 1)
    return jnp.where(rule(row) == col, value, 0.0).astype(BF16)


def to_phase(i):
    return ((i >> 2) & 3) * 64 + (i >> 4) * 4 + (i & 3)


def from_phase(i):
    return (i & ~63) + ((i >> 2) & 3) * 16 + ((i >> 4) & 3) * 4 + (i & 3)


def swap_phase(i):
    return (i & ~15) + (i & 3) * 4 + ((i >> 2) & 3)


def convolve(tap, rows, weight):
    parts = [tap(u, w).reshape(rows, 128) for u in range(3) for w in range(3)]
    return jnp.dot(jnp.concatenate(parts, axis=1), weight[...], preferred_element_type=F32)


def kernel(
    x_hbm, k1, b1, k2, b2, out_hbm,
    flat, xpad, e, m, plane, cross, bridge, spad, p_in, p_swap, p_out,
    in_sem, out_sem, halo_send, halo_recv, row_send, row_recv,
    plane_send, plane_recv, cross_send, cross_recv, e_sem, m_sem, bridge_send, bridge_recv,
):
    r, c = lax.axis_index("row"), lax.axis_index("col")
    y, x, core = r // 8, c // 2, r % 2
    z2, z1, z0 = (r // 4) % 2, (r // 2) % 2, c % 2
    z = 4 * z2 + 2 * z1 + z0
    mine = 2 * z1 + core
    apart = (y - x + 4) % 4
    diag, far = apart == 0, apart == 2
    near = (apart == 1) | (apart == 3)
    side = jnp.where(apart == 1, 0, 1)
    detour, bridging = (z == 3) | (z == 6), (z == 0) | (z == 1)

    def load(s):
        rows = pl.ds(16 * s, 16)
        return pltpu.make_async_copy(x_hbm.at[rows], flat.at[rows], in_sem.at[s])

    def save(part, j):
        cols = pl.ds(64 * j + 16 * part, 16)
        return pltpu.make_async_copy(flat.at[:, cols], out_hbm.at[:, cols], out_sem.at[part, j])

    def there(dr, dc):
        return (r + dr >= 0) & (r + dr < 32) & (c + dc >= 0) & (c + dc < 8)

    def near_end(d, last):
        return pl.ds(1, last) if d == 0 else pl.ds(1 if d < 0 else last, 1)

    def far_end(d, last):
        return pl.ds(1, last) if d == 0 else pl.ds(last + 1 if d < 0 else 0, 1)

    def x_edge(n):
        dr, dc = SIDES[n]
        src = xpad.at[near_end(dr, 16), near_end(dc, 64)]
        dst = xpad.at[far_end(dr, 16), far_end(dc, 64)]
        return copy(src, dst, halo_send.at[0, n], halo_recv.at[0, n], (r + dr, c + dc))

    def s_edge(n):
        dr, dc = SIDES[n]
        if dc < 0:
            src, dst = spad.at[near_end(dr, 16), 1, 0], spad.at[far_end(dr, 16), 17, 3]
        else:
            src, dst = spad.at[near_end(dr, 16), 16, 3], spad.at[far_end(dr, 16), 0, 0]
        return copy(src, dst, halo_send.at[1, n], halo_recv.at[1, n], (r + dr, c + dc))

    def each(numbers, action):
        for n in numbers:
            @pl.when(there(*SIDES[n]))
            def _():
                action(n)

    def opposite(n):
        return SIDES.index((-SIDES[n][0], -SIDES[n][1]))

    def s_row(n, line):
        src, dst = (1, 17) if n == 0 else (16, 0)
        return copy(
            spad.at[src, line + 1], spad.at[dst, line + 1],
            row_send.at[n, line], row_recv.at[n, line], (r + SIDES[n][0], c),
        )

    def copy(src, dst, send, recv, device):
        return pltpu.make_async_remote_copy(src, dst, send, recv, device_id=device, device_id_type=MESH)

    def chip(to_x, to_y):
        return (r - 8 * y + 8 * to_y, c - 2 * x + 2 * to_x)

    def to_mirror(line):
        return copy(e.at[line], plane.at[line], plane_send.at[line], plane_recv.at[line], chip(y, x))

    def to_corner(line):
        return copy(e.at[line], cross.at[side, line], plane_send.at[line], cross_recv.at[side, line], chip(x, x))

    def pass_on(line, n):
        to_x = (x + 1 + 2 * n) % 4
        return copy(cross.at[n, line], plane.at[line], cross_send.at[n, line], plane_recv.at[line], chip(to_x, y))

    def at_corner(line, n):
        return copy(cross.at[n, line], cross.at[n, line], cross_send.at[n, line], cross_recv.at[n, line], (r, c))

    def stays(k):
        return (z0 == z2) & (k == mine)

    def upright(src, line, k, dst, recv, device):
        return copy(src.at[line, pl.ds(16 * k, 16)], dst, e_sem.at[line, k], recv, device)

    def spread(line, src):
        for kk in range(4):
            k = (kk + mine) % 4
            around = detour & (k // 2 == 1) & (line % 2 == 1)
            half, low = line // 2, k % 2

            @pl.when(jnp.logical_not(stays(k)) & jnp.logical_not(around))
            def _():
                to = (8 * y + 4 * z0 + k, 2 * x + z2)
                upright(src, line, k, m.at[line, mine], m_sem.at[line, mine], to).start()

            @pl.when(stays(k))
            def _():
                m[line, mine] = src[line, pl.ds(16 * k, 16)]

            @pl.when(around)
            def _():
                to = (8 * y + core, 2 * x + jnp.where(z == 3, 0, 1))
                upright(src, line, k, bridge.at[half, low], bridge_recv.at[half, low], to).start()

    def bridge_on(half, low):
        to = (8 * y + jnp.where(z == 0, 6, 2) + low, 2 * x + jnp.where(z == 0, 0, 1))
        dst, recv = m.at[2 * half + 1, 2 + core], m_sem.at[2 * half + 1, 2 + core]
        return copy(bridge.at[half, low], dst, bridge_send.at[half, low], recv, to)

    def at_bridge(half, low):
        here = bridge.at[half, low]
        return copy(here, here, bridge_send.at[half, low], bridge_recv.at[half, low], (r, c))

    def route(line):
        @pl.when(diag)
        def _():
            for n in range(2):
                at_corner(line, n).wait_recv()
                pass_on(line, n).start()

        @pl.when(jnp.logical_not(diag))
        def _():
            to_mirror(line).wait_recv()
            spread(line, plane)

    def cross_over(line):
        @pl.when(bridging & (line % 2 == 1))
        def _():
            for low in range(2):
                at_bridge(line // 2, low).wait_recv()
                bridge_on(line // 2, low).start()

    def arrived(line, j):
        return upright(e, line, j, m.at[line, j], m_sem.at[line, j], (r, c))

    def first(line):
        for g in range(2):
            v = convolve(lambda u, w: xpad[line + u, pl.ds(32 * g + w, 32)], 512, k1) + b1[...]
            v = jnp.where(v > 0, v, jnp.exp(jnp.minimum(v, 0.0)) - 1.0)
            e[line, pl.ds(32 * g, 32)] = v.astype(BF16).reshape(32, 16, 128)

        @pl.when(near)
        def _():
            to_corner(line).start()

        @pl.when(far)
        def _():
            to_mirror(line).start()

        @pl.when(diag)
        def _():
            spread(line, e)

    def symmetrize(line):
        for j in range(4):
            @pl.when(jnp.logical_not(stays(j)))
            def _():
                arrived(line, j).wait_recv()

        for j in range(4):
            moved = jnp.dot(p_swap[...], m[line, j].reshape(256, 128), preferred_element_type=F32)
            own = e[:, 16 * j + line].reshape(256, 128).astype(F32)
            spad[pl.ds(1, 16), line + 1, j] = (0.5 * own + moved).astype(BF16).reshape(16, 16, 128)
        each((0, 1), lambda n: s_row(n, line).start())

    def rows_in(line):
        each((0, 1), lambda n: s_row(opposite(n), line).wait_recv())

    def second(line):
        for g in range(2):
            v = convolve(lambda u, w: spad[pl.ds(8 * g + u, 8), line + w], 512, k2) + b2[...]
            v = v + spad[pl.ds(8 * g + 1, 8), line + 1].reshape(512, 128).astype(F32)
            v = v.astype(BF16).reshape(8, 4, 16, 128)
            for j in range(4):
                xpad[pl.ds(8 * g, 8), 16 * j + line] = v[:, j]

    def natural(part):
        for j in range(4):
            for g in range(4):
                block = xpad[pl.ds(4 * g, 4), pl.ds(16 * j + 4 * part, 4)].reshape(256, 128)
                moved = jnp.dot(p_out[...], block, preferred_element_type=F32).astype(BF16)
                flat[pl.ds(16 * g, 16), pl.ds(64 * j + 16 * part, 16)] = moved.reshape(16, 16, 128)
            save(part, j).start()

    def at(step):
        return (step + 1) % LINES

    for s in range(4):
        load(s).start()
    p_in[...] = select(to_phase, 1.0)
    p_swap[...] = select(swap_phase, 0.5)
    p_out[...] = select(from_phase, 1.0)
    for cond, line in ((r == 0, 0), (r == 31, 17)):
        @pl.when(cond)
        def _():
            xpad[line] = jnp.zeros((66, 16, 128), BF16)
            spad[line] = jnp.zeros((18, 4, 16, 128), BF16)
    for cond, line, group, j in ((c == 0, 0, 0, 0), (c == 7, 65, 17, 3)):
        @pl.when(cond)
        def _():
            xpad[:, line] = jnp.zeros((18, 16, 128), BF16)
            spad[:, group, j] = jnp.zeros((18, 16, 128), BF16)

    def enter(line, groups):
        for g in groups:
            rows = flat[pl.ds(4 * line, 4), pl.ds(64 * g, 64)].reshape(256, 128)
            moved = jnp.dot(p_in[...], rows, preferred_element_type=F32).astype(BF16)
            xpad[line + 1, pl.ds(1 + 16 * g, 16)] = moved.reshape(16, 16, 128)

    for s in range(4):
        load(s).wait()

        @pl.loop(4 * s, 4 * s + 4)
        def _(line):
            enter(line, (0, 3))

    each((2, 3), lambda n: x_edge(n).start())

    @pl.loop(0, LINES)
    def _(line):
        enter(line, (1, 2))

    each((0, 1, 4, 5, 6, 7), lambda n: x_edge(n).start())
    each((2, 3), lambda n: x_edge(opposite(n)).wait_recv())

    @pl.loop(0, 2 * LINES)
    def _(t):
        @pl.when((t >= ROUTE) & (t < ROUTE + LINES))
        def _():
            route(at(t - ROUTE))

        @pl.when((t >= ROUTE + LAG) & (t < ROUTE + LAG + LINES))
        def _():
            cross_over(at(t - ROUTE - LAG))

        @pl.when(t < LINES)
        def _():
            @pl.when(t == LINES - 2)
            def _():
                each((0, 1, 4, 5, 6, 7), lambda n: x_edge(opposite(n)).wait_recv())
                each(range(8), lambda n: x_edge(n).wait_send())

            first(at(t))

        @pl.when(t >= LINES)
        def _():
            symmetrize(at(t - LINES))

        @pl.when(t == 2 * LINES - 2)
        def _():
            each((3, 5, 7), lambda n: s_edge(n).start())

        @pl.when(t == 2 * LINES - 1)
        def _():
            each((2, 4, 6), lambda n: s_edge(n).start())

        @pl.when(t > LINES)
        def _():
            rows_in(at(t - LINES - 1))

        @pl.when(t > LINES + 2)
        def _():
            second(at(t - LINES - 2))

        @pl.when((t == LINES + 9) | (t == LINES + 13))
        def _():
            natural((t - LINES - 5) // 4)

    rows_in(0)
    each((2, 3, 4, 5, 6, 7), lambda n: s_edge(opposite(n)).wait_recv())
    spad[:, 0, pl.ds(1, 3)] = spad[:, 16, pl.ds(0, 3)]
    spad[:, 17, pl.ds(0, 3)] = spad[:, 1, pl.ds(1, 3)]
    for line in (15, 0, 1):
        second(line)
        if line == 15:
            natural(3)
    natural(0)
    each(range(2, 8), lambda n: s_edge(n).wait_send())

    @pl.loop(0, LINES)
    def _(line):
        each((0, 1), lambda n: s_row(n, line).wait_send())
        for k in range(4):
            @pl.when(jnp.logical_not(stays(k)))
            def _():
                arrived(line, k).wait_send()

        @pl.when(diag)
        def _():
            for n in range(2):
                pass_on(line, n).wait_send()

        @pl.when(jnp.logical_not(diag))
        def _():
            to_mirror(line).wait_send()

        @pl.when(bridging & (line % 2 == 1))
        def _():
            for low in range(2):
                bridge_on(line // 2, low).wait_send()

    for part in range(4):
        for j in range(4):
            save(part, j).wait()


def body(activation, kernel_one, bias_one, kernel_two, bias_two):
    vmem, hbm = pl.BlockSpec(memory_space=pltpu.VMEM), pl.BlockSpec(memory_space=pl.ANY)
    dma = pltpu.SemaphoreType.DMA
    return pl.pallas_call(
        kernel,
        out_shape=jax.ShapeDtypeStruct(activation.shape, BF16),
        in_specs=[hbm, vmem, vmem, vmem, vmem],
        out_specs=hbm,
        scratch_shapes=[
            pltpu.VMEM((64, 256, 128), BF16),
            pltpu.VMEM((18, 66, 16, 128), BF16),
            pltpu.VMEM((16, 64, 16, 128), BF16),
            pltpu.VMEM((16, 4, 16, 16, 128), BF16),
            pltpu.VMEM((16, 64, 16, 128), BF16),
            pltpu.VMEM((2, 16, 64, 16, 128), BF16),
            pltpu.VMEM((8, 2, 16, 16, 128), BF16),
            pltpu.VMEM((18, 18, 4, 16, 128), BF16),
            pltpu.VMEM((256, 256), BF16),
            pltpu.VMEM((256, 256), BF16),
            pltpu.VMEM((256, 256), BF16),
            dma((4,)),
            dma((4, 4)),
            dma((2, 8)),
            dma((2, 8)),
            dma((2, 16)),
            dma((2, 16)),
            dma((16,)),
            dma((16,)),
            dma((2, 16)),
            dma((2, 16)),
            dma((16, 4)),
            dma((16, 4)),
            dma((8, 2)),
            dma((8, 2)),
        ],
        compiler_params=pltpu.CompilerParams(has_side_effects=True, vmem_limit_bytes=60 << 20),
        name="resblock",
    )(
        activation,
        kernel_one.reshape(1152, 128),
        bias_one.reshape(1, 128),
        kernel_two.reshape(1152, 128),
        bias_two.reshape(1, 128),
    )


def solution(mesh):
    in_specs = (P("row", "col", None), P(), P(), P(), P())
    out_specs = P("row", "col", None)
    return jax.shard_map(body, mesh=mesh, in_specs=in_specs, out_specs=out_specs, check_vma=False)
```

```python
import functools

import jax
import jax.numpy as jnp
from jax import lax
from jax.experimental import pallas as pl
from jax.experimental.pallas import tpu as pltpu
from jax.sharding import PartitionSpec as P

MESH = pl.DeviceIdType.MESH
F32, BF16 = jnp.float32, jnp.bfloat16
LINES = 16
LAG = 3
ROUTE = 3
SYM = 16
SIDES = ((-1, 0), (1, 0), (0, -1), (0, 1), (-1, -1), (-1, 1), (1, -1), (1, 1))


def select(rule, value):
    row = lax.broadcasted_iota(jnp.int32, (256, 256), 0)
    col = lax.broadcasted_iota(jnp.int32, (256, 256), 1)
    return jnp.where(rule(row) == col, value, 0.0).astype(BF16)


def to_phase(i):
    return ((i >> 2) & 3) * 64 + (i >> 4) * 4 + (i & 3)


def from_phase(i):
    return (i & ~63) + ((i >> 2) & 3) * 16 + ((i >> 4) & 3) * 4 + (i & 3)


def swap_phase(i):
    return (i & ~15) + (i & 3) * 4 + ((i >> 2) & 3)


def convolve(tap, rows, weight):
    parts = [tap(u, w).reshape(rows, 128) for u in range(3) for w in range(3)]
    return jnp.dot(jnp.concatenate(parts, axis=1), weight[...], preferred_element_type=F32)


def kernel(
    x_hbm, k1, b1, k2, b2, out_hbm,
    flat, xpad, e, m, plane, cross, bridge, spad, p_in, p_swap, p_out,
    in_sem, out_sem, halo_send, halo_recv, row_send, row_recv,
    plane_send, plane_recv, cross_send, cross_recv, e_sem, m_sem, bridge_send, bridge_recv,
):
    r, c = lax.axis_index("row"), lax.axis_index("col")
    y, x, core = r // 8, c // 2, r % 2
    z2, z1, z0 = (r // 4) % 2, (r // 2) % 2, c % 2
    z = 4 * z2 + 2 * z1 + z0
    mine = 2 * z1 + core
    apart = (y - x + 4) % 4
    diag, far = apart == 0, apart == 2
    near = (apart == 1) | (apart == 3)
    side = jnp.where(apart == 1, 0, 1)
    detour, bridging = (z == 3) | (z == 6), (z == 0) | (z == 1)

    def load(s):
        rows = pl.ds(16 * s, 16)
        return pltpu.make_async_copy(x_hbm.at[rows], flat.at[rows], in_sem.at[s])

    def save(g):
        rows = pl.ds(16 * g, 16)
        return pltpu.make_async_copy(flat.at[rows], out_hbm.at[rows], out_sem.at[g])

    def there(dr, dc):
        return (r + dr >= 0) & (r + dr < 32) & (c + dc >= 0) & (c + dc < 8)

    def near_end(d, last):
        return pl.ds(1, last) if d == 0 else pl.ds(1 if d < 0 else last, 1)

    def far_end(d, last):
        return pl.ds(1, last) if d == 0 else pl.ds(last + 1 if d < 0 else 0, 1)

    def x_edge(n):
        dr, dc = SIDES[n]
        src = xpad.at[near_end(dr, 16), near_end(dc, 64)]
        dst = xpad.at[far_end(dr, 16), far_end(dc, 64)]
        return copy(src, dst, halo_send.at[0, n], halo_recv.at[0, n], (r + dr, c + dc))

    def s_edge(n):
        dr, dc = SIDES[n]
        if dc < 0:
            src, dst = spad.at[near_end(dr, 16), 1, 0], spad.at[far_end(dr, 16), 17, 3]
        else:
            src, dst = spad.at[near_end(dr, 16), 16, 3], spad.at[far_end(dr, 16), 0, 0]
        return copy(src, dst, halo_send.at[1, n], halo_recv.at[1, n], (r + dr, c + dc))

    def each(numbers, action):
        for n in numbers:
            @pl.when(there(*SIDES[n]))
            def _():
                action(n)

    def opposite(n):
        return SIDES.index((-SIDES[n][0], -SIDES[n][1]))

    def s_row(n, line):
        src, dst = (1, 17) if n == 0 else (16, 0)
        return copy(
            spad.at[src, line + 1], spad.at[dst, line + 1],
            row_send.at[n, line], row_recv.at[n, line], (r + SIDES[n][0], c),
        )

    def copy(src, dst, send, recv, device):
        return pltpu.make_async_remote_copy(src, dst, send, recv, device_id=device, device_id_type=MESH)

    def chip(to_x, to_y):
        return (r - 8 * y + 8 * to_y, c - 2 * x + 2 * to_x)

    def to_mirror(line):
        return copy(e.at[line], plane.at[line], plane_send.at[line], plane_recv.at[line], chip(y, x))

    def to_corner(line):
        return copy(e.at[line], cross.at[side, line], plane_send.at[line], cross_recv.at[side, line], chip(x, x))

    def pass_on(line, n):
        to_x = (x + 1 + 2 * n) % 4
        return copy(cross.at[n, line], plane.at[line], cross_send.at[n, line], plane_recv.at[line], chip(to_x, y))

    def at_corner(line, n):
        return copy(cross.at[n, line], cross.at[n, line], cross_send.at[n, line], cross_recv.at[n, line], (r, c))

    def stays(k):
        return (z0 == z2) & (k == mine)

    def upright(src, line, k, dst, recv, device):
        return copy(src.at[line, pl.ds(16 * k, 16)], dst, e_sem.at[line, k], recv, device)

    def spread(line, src):
        for kk in range(4):
            k = (kk + mine) % 4
            around = detour & (k // 2 == 1) & (line % 2 == 1)
            half, low = line // 2, k % 2

            @pl.when(jnp.logical_not(stays(k)) & jnp.logical_not(around))
            def _():
                to = (8 * y + 4 * z0 + k, 2 * x + z2)
                upright(src, line, k, m.at[line, mine], m_sem.at[line, mine], to).start()

            @pl.when(stays(k))
            def _():
                m[line, mine] = src[line, pl.ds(16 * k, 16)]

            @pl.when(around)
            def _():
                to = (8 * y + core, 2 * x + jnp.where(z == 3, 0, 1))
                upright(src, line, k, bridge.at[half, low], bridge_recv.at[half, low], to).start()

    def bridge_on(half, low):
        to = (8 * y + jnp.where(z == 0, 6, 2) + low, 2 * x + jnp.where(z == 0, 0, 1))
        dst, recv = m.at[2 * half + 1, 2 + core], m_sem.at[2 * half + 1, 2 + core]
        return copy(bridge.at[half, low], dst, bridge_send.at[half, low], recv, to)

    def at_bridge(half, low):
        here = bridge.at[half, low]
        return copy(here, here, bridge_send.at[half, low], bridge_recv.at[half, low], (r, c))

    def route(line):
        @pl.when(diag)
        def _():
            for n in range(2):
                at_corner(line, n).wait_recv()
                pass_on(line, n).start()

        @pl.when(jnp.logical_not(diag))
        def _():
            to_mirror(line).wait_recv()
            spread(line, plane)

    def cross_over(line):
        @pl.when(bridging & (line % 2 == 1))
        def _():
            for low in range(2):
                at_bridge(line // 2, low).wait_recv()
                bridge_on(line // 2, low).start()

    def arrived(line, j):
        return upright(e, line, j, m.at[line, j], m_sem.at[line, j], (r, c))

    def first(line):
        for g in range(2):
            v = convolve(lambda u, w: xpad[line + u, pl.ds(32 * g + w, 32)], 512, k1) + b1[...]
            v = jnp.where(v > 0, v, jnp.exp(jnp.minimum(v, 0.0)) - 1.0)
            e[line, pl.ds(32 * g, 32)] = v.astype(BF16).reshape(32, 16, 128)

        @pl.when(near)
        def _():
            to_corner(line).start()

        @pl.when(far)
        def _():
            to_mirror(line).start()

        @pl.when(diag)
        def _():
            spread(line, e)

    def symmetrize(line):
        for j in range(4):
            @pl.when(jnp.logical_not(stays(j)))
            def _():
                arrived(line, j).wait_recv()

        for j in range(4):
            moved = jnp.dot(p_swap[...], m[line, j].reshape(256, 128), preferred_element_type=F32)
            own = e[:, 16 * j + line].reshape(256, 128).astype(F32)
            spad[pl.ds(1, 16), line + 1, j] = (0.5 * own + moved).astype(BF16).reshape(16, 16, 128)
        each((0, 1), lambda n: s_row(n, line).start())

    def rows_in(line):
        each((0, 1), lambda n: s_row(opposite(n), line).wait_recv())

    def finish(tap, center, rows):
        v = convolve(tap, rows, k2) + b2[...]
        return (v + center.reshape(rows, 128).astype(F32)).astype(BF16)

    def second(line):
        for g in range(2):
            top = 7 * g + 1
            v = finish(lambda u, w: spad[pl.ds(top + u, 7), line + w], spad[pl.ds(top + 1, 7), line + 1], 448)
            v = v.reshape(7, 4, 16, 128)
            for j in range(4):
                xpad[pl.ds(top, 7), 16 * j + line] = v[:, j]

    def second_edge(row):
        for g in range(2):
            v = finish(lambda u, w: spad[row + u, pl.ds(8 * g + w, 8)], spad[row + 1, pl.ds(8 * g + 1, 8)], 512)
            v = v.reshape(8, 4, 16, 128)
            for j in range(4):
                xpad[row, pl.ds(16 * j + 8 * g, 8)] = v[:, j]

    def natural(part, g):
        for j in range(4):
            block = xpad[pl.ds(4 * g, 4), pl.ds(16 * j + 4 * part, 4)].reshape(256, 128)
            moved = jnp.dot(p_out[...], block, preferred_element_type=F32).astype(BF16)
            flat[pl.ds(16 * g, 16), pl.ds(64 * j + 16 * part, 16)] = moved.reshape(16, 16, 128)

    def at(step):
        return (step + 1) % LINES

    for s in range(4):
        load(s).start()
    p_in[...] = select(to_phase, 1.0)
    p_swap[...] = select(swap_phase, 0.5)
    p_out[...] = select(from_phase, 1.0)
    for cond, line in ((r == 0, 0), (r == 31, 17)):
        @pl.when(cond)
        def _():
            xpad[line] = jnp.zeros((66, 16, 128), BF16)
            spad[line] = jnp.zeros((18, 4, 16, 128), BF16)
    for cond, line, group, j in ((c == 0, 0, 0, 0), (c == 7, 65, 17, 3)):
        @pl.when(cond)
        def _():
            xpad[:, line] = jnp.zeros((18, 16, 128), BF16)
            spad[:, group, j] = jnp.zeros((18, 16, 128), BF16)

    def enter(line, groups):
        for g in groups:
            rows = flat[pl.ds(4 * line, 4), pl.ds(64 * g, 64)].reshape(256, 128)
            moved = jnp.dot(p_in[...], rows, preferred_element_type=F32).astype(BF16)
            xpad[line + 1, pl.ds(1 + 16 * g, 16)] = moved.reshape(16, 16, 128)

    for s in range(4):
        load(s).wait()

        @pl.loop(4 * s, 4 * s + 4)
        def _(line):
            enter(line, (0, 3))

    each((2, 3), lambda n: x_edge(n).start())

    @pl.loop(0, LINES)
    def _(line):
        enter(line, (1, 2))

    each((0, 1, 4, 5, 6, 7), lambda n: x_edge(n).start())
    each((2, 3), lambda n: x_edge(opposite(n)).wait_recv())

    @pl.loop(0, SYM + LINES)
    def _(t):
        @pl.when((t >= ROUTE) & (t < ROUTE + LINES))
        def _():
            route(at(t - ROUTE))

        @pl.when((t >= ROUTE + LAG) & (t < ROUTE + LAG + LINES))
        def _():
            cross_over(at(t - ROUTE - LAG))

        @pl.when(t < LINES)
        def _():
            @pl.when(t == LINES - 2)
            def _():
                each((0, 1, 4, 5, 6, 7), lambda n: x_edge(opposite(n)).wait_recv())
                each(range(8), lambda n: x_edge(n).wait_send())

            first(at(t))

        @pl.when(t >= SYM)
        def _():
            symmetrize(at(t - SYM))

        @pl.when(t == SYM + LINES - 2)
        def _():
            each((3, 5, 7), lambda n: s_edge(n).start())

        @pl.when(t == SYM + LINES - 1)
        def _():
            each((2, 4, 6), lambda n: s_edge(n).start())

        @pl.when(t > SYM + 2)
        def _():
            second(at(t - SYM - 2))

        @pl.when((t == SYM + 9) | (t == SYM + 13))
        def _():
            for g in (1, 2):
                natural((t - SYM - 5) // 4, g)

    each((2, 3, 4, 5, 6, 7), lambda n: s_edge(opposite(n)).wait_recv())
    spad[pl.ds(1, 16), 0, pl.ds(1, 3)] = spad[pl.ds(1, 16), 16, pl.ds(0, 3)]
    spad[pl.ds(1, 16), 17, pl.ds(0, 3)] = spad[pl.ds(1, 16), 1, pl.ds(1, 3)]
    for line in (15, 0, 1):
        second(line)
    for g in (1, 2):
        for part in (0, 3):
            natural(part, g)
        save(g).start()

    @pl.loop(0, LINES)
    def _(line):
        rows_in(line)

    for row in (0, 15):
        spad[row + (row > 0) * 2, 0, pl.ds(1, 3)] = spad[row + (row > 0) * 2, 16, pl.ds(0, 3)]
        spad[row + (row > 0) * 2, 17, pl.ds(0, 3)] = spad[row + (row > 0) * 2, 1, pl.ds(1, 3)]
        second_edge(row)
        for part in range(4):
            natural(part, row // 5)
        save(row // 5).start()
    each(range(2, 8), lambda n: s_edge(n).wait_send())

    @pl.loop(0, LINES)
    def _(line):
        each((0, 1), lambda n: s_row(n, line).wait_send())
        for k in range(4):
            @pl.when(jnp.logical_not(stays(k)))
            def _():
                arrived(line, k).wait_send()

        @pl.when(diag)
        def _():
            for n in range(2):
                pass_on(line, n).wait_send()

        @pl.when(jnp.logical_not(diag))
        def _():
            to_mirror(line).wait_send()

        @pl.when(bridging & (line % 2 == 1))
        def _():
            for low in range(2):
                bridge_on(line // 2, low).wait_send()

    for g in range(4):
        save(g).wait()


def body(activation, kernel_one, bias_one, kernel_two, bias_two):
    vmem, hbm = pl.BlockSpec(memory_space=pltpu.VMEM), pl.BlockSpec(memory_space=pl.ANY)
    dma = pltpu.SemaphoreType.DMA
    return pl.pallas_call(
        kernel,
        out_shape=jax.ShapeDtypeStruct(activation.shape, BF16),
        in_specs=[hbm, vmem, vmem, vmem, vmem],
        out_specs=hbm,
        scratch_shapes=[
            pltpu.VMEM((64, 256, 128), BF16),
            pltpu.VMEM((18, 66, 16, 128), BF16),
            pltpu.VMEM((16, 64, 16, 128), BF16),
            pltpu.VMEM((16, 4, 16, 16, 128), BF16),
            pltpu.VMEM((16, 64, 16, 128), BF16),
            pltpu.VMEM((2, 16, 64, 16, 128), BF16),
            pltpu.VMEM((8, 2, 16, 16, 128), BF16),
            pltpu.VMEM((18, 18, 4, 16, 128), BF16),
            pltpu.VMEM((256, 256), BF16),
            pltpu.VMEM((256, 256), BF16),
            pltpu.VMEM((256, 256), BF16),
            dma((4,)),
            dma((4,)),
            dma((2, 8)),
            dma((2, 8)),
            dma((2, 16)),
            dma((2, 16)),
            dma((16,)),
            dma((16,)),
            dma((2, 16)),
            dma((2, 16)),
            dma((16, 4)),
            dma((16, 4)),
            dma((8, 2)),
            dma((8, 2)),
        ],
        compiler_params=pltpu.CompilerParams(has_side_effects=True, vmem_limit_bytes=60 << 20),
        name="resblock",
    )(
        activation,
        kernel_one.reshape(1152, 128),
        bias_one.reshape(1, 128),
        kernel_two.reshape(1152, 128),
        bias_two.reshape(1, 128),
    )


def solution(mesh):
    in_specs = (P("row", "col", None), P(), P(), P(), P())
    out_specs = P("row", "col", None)
    return jax.shard_map(body, mesh=mesh, in_specs=in_specs, out_specs=out_specs, check_vma=False)
```

```python
import functools

import jax
import jax.numpy as jnp
from jax import lax
from jax.experimental import pallas as pl
from jax.experimental.pallas import tpu as pltpu
from jax.sharding import PartitionSpec as P

MESH = pl.DeviceIdType.MESH
F32, BF16 = jnp.float32, jnp.bfloat16
LINES = 16
LAG = 5
ROUTE = 4
SYM = 16
SIDES = ((-1, 0), (1, 0), (0, -1), (0, 1), (-1, -1), (-1, 1), (1, -1), (1, 1))


def select(rule, value):
    row = lax.broadcasted_iota(jnp.int32, (256, 256), 0)
    col = lax.broadcasted_iota(jnp.int32, (256, 256), 1)
    return jnp.where(rule(row) == col, value, 0.0).astype(BF16)


def to_phase(i):
    return ((i >> 2) & 3) * 64 + (i >> 4) * 4 + (i & 3)


def from_phase(i):
    return (i & ~63) + ((i >> 2) & 3) * 16 + ((i >> 4) & 3) * 4 + (i & 3)


def swap_phase(i):
    return (i & ~15) + (i & 3) * 4 + ((i >> 2) & 3)


def convolve(tap, rows, weight):
    parts = [tap(u, w).reshape(rows, 128) for u in range(3) for w in range(3)]
    return jnp.dot(jnp.concatenate(parts, axis=1), weight[...], preferred_element_type=F32)


def kernel(
    x_hbm, k1, b1, k2, b2, out_hbm,
    flat, xpad, e, m, plane, cross, bridge, spad, p_in, p_swap, p_out,
    in_sem, out_sem, halo_send, halo_recv, row_send, row_recv,
    plane_send, plane_recv, cross_send, cross_recv, e_sem, m_sem, bridge_send, bridge_recv,
):
    r, c = lax.axis_index("row"), lax.axis_index("col")
    y, x, core = r // 8, c // 2, r % 2
    z2, z1, z0 = (r // 4) % 2, (r // 2) % 2, c % 2
    z = 4 * z2 + 2 * z1 + z0
    mine = 2 * z1 + core
    apart = (y - x + 4) % 4
    diag, far = apart == 0, apart == 2
    near = (apart == 1) | (apart == 3)
    side = jnp.where(apart == 1, 0, 1)
    detour, bridging = (z == 3) | (z == 6), (z == 0) | (z == 1)

    def load(s):
        rows = pl.ds(16 * s, 16)
        return pltpu.make_async_copy(x_hbm.at[rows], flat.at[rows], in_sem.at[s])

    def save(g):
        rows = pl.ds(16 * g, 16)
        return pltpu.make_async_copy(flat.at[rows], out_hbm.at[rows], out_sem.at[g])

    def there(dr, dc):
        return (r + dr >= 0) & (r + dr < 32) & (c + dc >= 0) & (c + dc < 8)

    def near_end(d, last):
        return pl.ds(1, last) if d == 0 else pl.ds(1 if d < 0 else last, 1)

    def far_end(d, last):
        return pl.ds(1, last) if d == 0 else pl.ds(last + 1 if d < 0 else 0, 1)

    def x_edge(n):
        dr, dc = SIDES[n]
        src = xpad.at[near_end(dr, 16), near_end(dc, 64)]
        dst = xpad.at[far_end(dr, 16), far_end(dc, 64)]
        return copy(src, dst, halo_send.at[0, n], halo_recv.at[0, n], (r + dr, c + dc))

    def s_edge(n):
        dr, dc = SIDES[n]
        if dc < 0:
            src, dst = spad.at[near_end(dr, 16), 1, 0], spad.at[far_end(dr, 16), 17, 3]
        else:
            src, dst = spad.at[near_end(dr, 16), 16, 3], spad.at[far_end(dr, 16), 0, 0]
        return copy(src, dst, halo_send.at[1, n], halo_recv.at[1, n], (r + dr, c + dc))

    def each(numbers, action):
        for n in numbers:
            @pl.when(there(*SIDES[n]))
            def _():
                action(n)

    def opposite(n):
        return SIDES.index((-SIDES[n][0], -SIDES[n][1]))

    def s_row(n, line):
        src, dst = (1, 17) if n == 0 else (16, 0)
        return copy(
            spad.at[src, line + 1], spad.at[dst, line + 1],
            row_send.at[n, line], row_recv.at[n, line], (r + SIDES[n][0], c),
        )

    def copy(src, dst, send, recv, device):
        return pltpu.make_async_remote_copy(src, dst, send, recv, device_id=device, device_id_type=MESH)

    def chip(to_x, to_y):
        return (r - 8 * y + 8 * to_y, c - 2 * x + 2 * to_x)

    def to_mirror(line):
        return copy(e.at[line], plane.at[line], plane_send.at[line], plane_recv.at[line], chip(y, x))

    def to_corner(line):
        return copy(e.at[line], cross.at[side, line], plane_send.at[line], cross_recv.at[side, line], chip(x, x))

    def pass_on(line, n):
        to_x = (x + 1 + 2 * n) % 4
        return copy(cross.at[n, line], plane.at[line], cross_send.at[n, line], plane_recv.at[line], chip(to_x, y))

    def at_corner(line, n):
        return copy(cross.at[n, line], cross.at[n, line], cross_send.at[n, line], cross_recv.at[n, line], (r, c))

    def stays(k):
        return (z0 == z2) & (k == mine)

    def upright(src, line, k, dst, recv, device):
        return copy(src.at[line, pl.ds(16 * k, 16)], dst, e_sem.at[line, k], recv, device)

    def spread(line, src):
        for kk in range(4):
            k = (kk + mine) % 4
            around = detour & (k // 2 == 1) & (line % 2 == 1)
            half, low = line // 2, k % 2

            @pl.when(jnp.logical_not(stays(k)) & jnp.logical_not(around))
            def _():
                to = (8 * y + 4 * z0 + k, 2 * x + z2)
                upright(src, line, k, m.at[line, mine], m_sem.at[line, mine], to).start()

            @pl.when(stays(k))
            def _():
                m[line, mine] = src[line, pl.ds(16 * k, 16)]

            @pl.when(around)
            def _():
                to = (8 * y + core, 2 * x + jnp.where(z == 3, 0, 1))
                upright(src, line, k, bridge.at[half, low], bridge_recv.at[half, low], to).start()

    def bridge_on(half, low):
        to = (8 * y + jnp.where(z == 0, 6, 2) + low, 2 * x + jnp.where(z == 0, 0, 1))
        dst, recv = m.at[2 * half + 1, 2 + core], m_sem.at[2 * half + 1, 2 + core]
        return copy(bridge.at[half, low], dst, bridge_send.at[half, low], recv, to)

    def at_bridge(half, low):
        here = bridge.at[half, low]
        return copy(here, here, bridge_send.at[half, low], bridge_recv.at[half, low], (r, c))

    def route(line):
        @pl.when(diag)
        def _():
            for n in range(2):
                at_corner(line, n).wait_recv()
                pass_on(line, n).start()

        @pl.when(jnp.logical_not(diag))
        def _():
            to_mirror(line).wait_recv()
            spread(line, plane)

    def cross_over(line):
        @pl.when(bridging & (line % 2 == 1))
        def _():
            for low in range(2):
                at_bridge(line // 2, low).wait_recv()
                bridge_on(line // 2, low).start()

    def arrived(line, j):
        return upright(e, line, j, m.at[line, j], m_sem.at[line, j], (r, c))

    def first(line):
        for g in range(2):
            v = convolve(lambda u, w: xpad[line + u, pl.ds(32 * g + w, 32)], 512, k1) + b1[...]
            v = jnp.where(v > 0, v, jnp.exp(jnp.minimum(v, 0.0)) - 1.0)
            e[line, pl.ds(32 * g, 32)] = v.astype(BF16).reshape(32, 16, 128)

        @pl.when(near)
        def _():
            to_corner(line).start()

        @pl.when(far)
        def _():
            to_mirror(line).start()

        @pl.when(diag)
        def _():
            spread(line, e)

    def symmetrize(line):
        for j in range(4):
            @pl.when(jnp.logical_not(stays(j)))
            def _():
                arrived(line, j).wait_recv()

        for j in range(4):
            moved = jnp.dot(p_swap[...], m[line, j].reshape(256, 128), preferred_element_type=F32)
            own = e[:, 16 * j + line].reshape(256, 128).astype(F32)
            spad[pl.ds(1, 16), line + 1, j] = (0.5 * own + moved).astype(BF16).reshape(16, 16, 128)
        each((0, 1), lambda n: s_row(n, line).start())

    def rows_in(line):
        each((0, 1), lambda n: s_row(opposite(n), line).wait_recv())

    def finish(tap, center, rows):
        v = convolve(tap, rows, k2) + b2[...]
        return (v + center.reshape(rows, 128).astype(F32)).astype(BF16)

    def second(line):
        for g in range(2):
            top = 7 * g + 1
            v = finish(lambda u, w: spad[pl.ds(top + u, 7), line + w], spad[pl.ds(top + 1, 7), line + 1], 448)
            v = v.reshape(7, 4, 16, 128)
            for j in range(4):
                xpad[pl.ds(top, 7), 16 * j + line] = v[:, j]

    def second_edge(row):
        for g in range(2):
            v = finish(lambda u, w: spad[row + u, pl.ds(8 * g + w, 8)], spad[row + 1, pl.ds(8 * g + 1, 8)], 512)
            v = v.reshape(8, 4, 16, 128)
            for j in range(4):
                xpad[row, pl.ds(16 * j + 8 * g, 8)] = v[:, j]

    def natural(part, g):
        for j in range(4):
            block = xpad[pl.ds(4 * g, 4), pl.ds(16 * j + 4 * part, 4)].reshape(256, 128)
            moved = jnp.dot(p_out[...], block, preferred_element_type=F32).astype(BF16)
            flat[pl.ds(16 * g, 16), pl.ds(64 * j + 16 * part, 16)] = moved.reshape(16, 16, 128)

    def at(step):
        return (step + 1) % LINES

    def zone(at_z, at_core):
        return (8 * y + 2 * (at_z // 2) + at_core, 2 * x + at_z % 2)

    up, down = (x + 1) % 4, (x + 3) % 4
    single = jnp.where(z == 3, 0, jnp.where(z == 6, 1, jnp.where(z == 0, 3, 6)))
    double = jnp.where(z == 3, 1, jnp.where(z == 6, 0, jnp.where(z == 0, 6, 3)))
    peers = [(there(*side), (r + side[0], c + side[1])) for side in SIDES]
    peers += [(far, chip(y, x)), (near, chip(x, x)), (near, chip(y, y))]
    peers += [(diag, chip(*to)) for to in ((x, up), (x, down), (up, x), (down, x))]
    peers += [(jnp.logical_not(stays(k)), (8 * y + 4 * z0 + k, 2 * x + z2)) for k in range(4)]
    peers += [(detour | bridging, zone(*to)) for to in ((single, core), (double, 0), (double, 1))]
    barrier = pltpu.get_barrier_semaphore()
    for cond, device in peers:
        @pl.when(cond)
        def _():
            pl.semaphore_signal(barrier, inc=1, device_id=device, device_id_type=MESH)

    for s in range(4):
        load(s).start()
    p_in[...] = select(to_phase, 1.0)
    p_swap[...] = select(swap_phase, 0.5)
    p_out[...] = select(from_phase, 1.0)
    for cond, line in ((r == 0, 0), (r == 31, 17)):
        @pl.when(cond)
        def _():
            xpad[line] = jnp.zeros((66, 16, 128), BF16)
            spad[line] = jnp.zeros((18, 4, 16, 128), BF16)
    for cond, line, group, j in ((c == 0, 0, 0, 0), (c == 7, 65, 17, 3)):
        @pl.when(cond)
        def _():
            xpad[:, line] = jnp.zeros((18, 16, 128), BF16)
            spad[:, group, j] = jnp.zeros((18, 16, 128), BF16)

    def enter(line, groups):
        for g in groups:
            rows = flat[pl.ds(4 * line, 4), pl.ds(64 * g, 64)].reshape(256, 128)
            moved = jnp.dot(p_in[...], rows, preferred_element_type=F32).astype(BF16)
            xpad[line + 1, pl.ds(1 + 16 * g, 16)] = moved.reshape(16, 16, 128)

    for s in range(4):
        load(s).wait()

        @pl.loop(4 * s, 4 * s + 4)
        def _(line):
            enter(line, (0, 3))

    pl.semaphore_wait(barrier, sum(cond.astype(jnp.int32) for cond, _ in peers))
    each((2, 3), lambda n: x_edge(n).start())

    @pl.loop(0, LINES)
    def _(line):
        enter(line, (1, 2))

    each((0, 1, 4, 5, 6, 7), lambda n: x_edge(n).start())
    each((2, 3), lambda n: x_edge(opposite(n)).wait_recv())

    @pl.loop(0, SYM + LINES)
    def _(t):
        @pl.when((t >= ROUTE) & (t < ROUTE + LINES))
        def _():
            route(at(t - ROUTE))

        @pl.when((t >= ROUTE + LAG) & (t < ROUTE + LAG + LINES))
        def _():
            cross_over(at(t - ROUTE - LAG))

        @pl.when(t < LINES)
        def _():
            @pl.when(t == LINES - 2)
            def _():
                each((0, 1, 4, 5, 6, 7), lambda n: x_edge(opposite(n)).wait_recv())
                each(range(8), lambda n: x_edge(n).wait_send())

            first(at(t))

        @pl.when(t >= SYM)
        def _():
            symmetrize(at(t - SYM))

        @pl.when(t == SYM + LINES - 2)
        def _():
            each((3, 5, 7), lambda n: s_edge(n).start())

        @pl.when(t == SYM + LINES - 1)
        def _():
            each((2, 4, 6), lambda n: s_edge(n).start())

        @pl.when(t > SYM + 2)
        def _():
            second(at(t - SYM - 2))

        @pl.when((t == SYM + 9) | (t == SYM + 13))
        def _():
            for g in (1, 2):
                natural((t - SYM - 5) // 4, g)

    each((2, 3, 4, 5, 6, 7), lambda n: s_edge(opposite(n)).wait_recv())
    spad[pl.ds(1, 16), 0, pl.ds(1, 3)] = spad[pl.ds(1, 16), 16, pl.ds(0, 3)]
    spad[pl.ds(1, 16), 17, pl.ds(0, 3)] = spad[pl.ds(1, 16), 1, pl.ds(1, 3)]
    for line in (15, 0, 1):
        second(line)
    for g in (1, 2):
        for part in (0, 3):
            natural(part, g)
        save(g).start()

    @pl.loop(0, LINES)
    def _(line):
        rows_in(line)

    for row in (0, 15):
        spad[row + (row > 0) * 2, 0, pl.ds(1, 3)] = spad[row + (row > 0) * 2, 16, pl.ds(0, 3)]
        spad[row + (row > 0) * 2, 17, pl.ds(0, 3)] = spad[row + (row > 0) * 2, 1, pl.ds(1, 3)]
        second_edge(row)
        for part in range(4):
            natural(part, row // 5)
        save(row // 5).start()
    each(range(2, 8), lambda n: s_edge(n).wait_send())

    @pl.loop(0, LINES)
    def _(line):
        each((0, 1), lambda n: s_row(n, line).wait_send())
        for k in range(4):
            @pl.when(jnp.logical_not(stays(k)))
            def _():
                arrived(line, k).wait_send()

        @pl.when(diag)
        def _():
            for n in range(2):
                pass_on(line, n).wait_send()

        @pl.when(jnp.logical_not(diag))
        def _():
            to_mirror(line).wait_send()

        @pl.when(bridging & (line % 2 == 1))
        def _():
            for low in range(2):
                bridge_on(line // 2, low).wait_send()

    for g in range(4):
        save(g).wait()


def body(activation, kernel_one, bias_one, kernel_two, bias_two):
    vmem, hbm = pl.BlockSpec(memory_space=pltpu.VMEM), pl.BlockSpec(memory_space=pl.ANY)
    dma = pltpu.SemaphoreType.DMA
    return pl.pallas_call(
        kernel,
        out_shape=jax.ShapeDtypeStruct(activation.shape, BF16),
        in_specs=[hbm, vmem, vmem, vmem, vmem],
        out_specs=hbm,
        scratch_shapes=[
            pltpu.VMEM((64, 256, 128), BF16),
            pltpu.VMEM((18, 66, 16, 128), BF16),
            pltpu.VMEM((16, 64, 16, 128), BF16),
            pltpu.VMEM((16, 4, 16, 16, 128), BF16),
            pltpu.VMEM((16, 64, 16, 128), BF16),
            pltpu.VMEM((2, 16, 64, 16, 128), BF16),
            pltpu.VMEM((8, 2, 16, 16, 128), BF16),
            pltpu.VMEM((18, 18, 4, 16, 128), BF16),
            pltpu.VMEM((256, 256), BF16),
            pltpu.VMEM((256, 256), BF16),
            pltpu.VMEM((256, 256), BF16),
            dma((4,)),
            dma((4,)),
            dma((2, 8)),
            dma((2, 8)),
            dma((2, 16)),
            dma((2, 16)),
            dma((16,)),
            dma((16,)),
            dma((2, 16)),
            dma((2, 16)),
            dma((16, 4)),
            dma((16, 4)),
            dma((8, 2)),
            dma((8, 2)),
        ],
        compiler_params=pltpu.CompilerParams(collective_id=0, has_side_effects=True, vmem_limit_bytes=60 << 20),
        name="resblock",
    )(
        activation,
        kernel_one.reshape(1152, 128),
        bias_one.reshape(1, 128),
        kernel_two.reshape(1152, 128),
        bias_two.reshape(1, 128),
    )


def solution(mesh):
    in_specs = (P("row", "col", None), P(), P(), P(), P())
    out_specs = P("row", "col", None)
    return jax.shard_map(body, mesh=mesh, in_specs=in_specs, out_specs=out_specs, check_vma=False)
```

```python
import functools

import jax
import jax.numpy as jnp
from jax import lax
from jax.experimental import pallas as pl
from jax.experimental.pallas import tpu as pltpu
from jax.sharding import PartitionSpec as P

MESH = pl.DeviceIdType.MESH
F32, BF16 = jnp.float32, jnp.bfloat16
LINES = 16
LAG = 5
ROUTE = 4
SYM = 16
SIDES = ((-1, 0), (1, 0), (0, -1), (0, 1), (-1, -1), (-1, 1), (1, -1), (1, 1))


def select(rule, value):
    row = lax.broadcasted_iota(jnp.int32, (256, 256), 0)
    col = lax.broadcasted_iota(jnp.int32, (256, 256), 1)
    return jnp.where(rule(row) == col, value, 0.0).astype(BF16)


def regroup(tiles):
    wide = [tile.astype(F32) for tile in tiles]
    parts = [jnp.concatenate([w[:, 4 * n : 4 * n + 4] for w in wide], axis=1).astype(BF16) for n in range(4)]
    return jnp.stack(parts, axis=1).reshape(16, 16, 128)


def swap_phase(i):
    return (i & ~15) + (i & 3) * 4 + ((i >> 2) & 3)


def convolve(tap, rows, weight):
    parts = [tap(u, w).reshape(rows, 128) for u in range(3) for w in range(3)]
    return jnp.dot(jnp.concatenate(parts, axis=1), weight[...], preferred_element_type=F32)


def kernel(
    x_hbm, k1, b1, k2, b2, out_hbm,
    flat, xpad, e, m, plane, cross, bridge, spad, p_swap,
    in_sem, out_sem, halo_send, halo_recv, row_send, row_recv,
    plane_send, plane_recv, cross_send, cross_recv, e_sem, m_sem, bridge_send, bridge_recv,
):
    r, c = lax.axis_index("row"), lax.axis_index("col")
    y, x, core = r // 8, c // 2, r % 2
    z2, z1, z0 = (r // 4) % 2, (r // 2) % 2, c % 2
    z = 4 * z2 + 2 * z1 + z0
    mine = 2 * z1 + core
    apart = (y - x + 4) % 4
    diag, far = apart == 0, apart == 2
    near = (apart == 1) | (apart == 3)
    side = jnp.where(apart == 1, 0, 1)
    detour, bridging = (z == 3) | (z == 6), (z == 0) | (z == 1)

    def load(s):
        rows = pl.ds(16 * s, 16)
        return pltpu.make_async_copy(x_hbm.at[rows], flat.at[rows], in_sem.at[s])

    def save(g):
        rows = pl.ds(16 * g, 16)
        return pltpu.make_async_copy(flat.at[rows], out_hbm.at[rows], out_sem.at[g])

    def there(dr, dc):
        return (r + dr >= 0) & (r + dr < 32) & (c + dc >= 0) & (c + dc < 8)

    def near_end(d, last):
        return pl.ds(1, last) if d == 0 else pl.ds(1 if d < 0 else last, 1)

    def far_end(d, last):
        return pl.ds(1, last) if d == 0 else pl.ds(last + 1 if d < 0 else 0, 1)

    def x_edge(n):
        dr, dc = SIDES[n]
        src = xpad.at[near_end(dr, 16), near_end(dc, 64)]
        dst = xpad.at[far_end(dr, 16), far_end(dc, 64)]
        return copy(src, dst, halo_send.at[0, n], halo_recv.at[0, n], (r + dr, c + dc))

    def s_edge(n):
        dr, dc = SIDES[n]
        if dc < 0:
            src, dst = spad.at[near_end(dr, 16), 1, 0], spad.at[far_end(dr, 16), 17, 3]
        else:
            src, dst = spad.at[near_end(dr, 16), 16, 3], spad.at[far_end(dr, 16), 0, 0]
        return copy(src, dst, halo_send.at[1, n], halo_recv.at[1, n], (r + dr, c + dc))

    def each(numbers, action):
        for n in numbers:
            @pl.when(there(*SIDES[n]))
            def _():
                action(n)

    def opposite(n):
        return SIDES.index((-SIDES[n][0], -SIDES[n][1]))

    def s_row(n, line):
        src, dst = (1, 17) if n == 0 else (16, 0)
        return copy(
            spad.at[src, line + 1], spad.at[dst, line + 1],
            row_send.at[n, line], row_recv.at[n, line], (r + SIDES[n][0], c),
        )

    def copy(src, dst, send, recv, device):
        return pltpu.make_async_remote_copy(src, dst, send, recv, device_id=device, device_id_type=MESH)

    def chip(to_x, to_y):
        return (r - 8 * y + 8 * to_y, c - 2 * x + 2 * to_x)

    def to_mirror(line):
        return copy(e.at[line], plane.at[line], plane_send.at[line], plane_recv.at[line], chip(y, x))

    def to_corner(line):
        return copy(e.at[line], cross.at[side, line], plane_send.at[line], cross_recv.at[side, line], chip(x, x))

    def pass_on(line, n):
        to_x = (x + 1 + 2 * n) % 4
        return copy(cross.at[n, line], plane.at[line], cross_send.at[n, line], plane_recv.at[line], chip(to_x, y))

    def at_corner(line, n):
        return copy(cross.at[n, line], cross.at[n, line], cross_send.at[n, line], cross_recv.at[n, line], (r, c))

    def stays(k):
        return (z0 == z2) & (k == mine)

    def upright(src, line, k, dst, recv, device):
        return copy(src.at[line, pl.ds(16 * k, 16)], dst, e_sem.at[line, k], recv, device)

    def spread(line, src):
        for kk in range(4):
            k = (kk + mine) % 4
            around = detour & (k // 2 == 1) & (line % 2 == 1)
            half, low = line // 2, k % 2

            @pl.when(jnp.logical_not(stays(k)) & jnp.logical_not(around))
            def _():
                to = (8 * y + 4 * z0 + k, 2 * x + z2)
                upright(src, line, k, m.at[line, mine], m_sem.at[line, mine], to).start()

            @pl.when(stays(k))
            def _():
                m[line, mine] = src[line, pl.ds(16 * k, 16)]

            @pl.when(around)
            def _():
                to = (8 * y + core, 2 * x + jnp.where(z == 3, 0, 1))
                upright(src, line, k, bridge.at[half, low], bridge_recv.at[half, low], to).start()

    def bridge_on(half, low):
        to = (8 * y + jnp.where(z == 0, 6, 2) + low, 2 * x + jnp.where(z == 0, 0, 1))
        dst, recv = m.at[2 * half + 1, 2 + core], m_sem.at[2 * half + 1, 2 + core]
        return copy(bridge.at[half, low], dst, bridge_send.at[half, low], recv, to)

    def at_bridge(half, low):
        here = bridge.at[half, low]
        return copy(here, here, bridge_send.at[half, low], bridge_recv.at[half, low], (r, c))

    def route(line):
        @pl.when(diag)
        def _():
            for n in range(2):
                at_corner(line, n).wait_recv()
                pass_on(line, n).start()

        @pl.when(jnp.logical_not(diag))
        def _():
            to_mirror(line).wait_recv()
            spread(line, plane)

    def cross_over(line):
        @pl.when(bridging & (line % 2 == 1))
        def _():
            for low in range(2):
                at_bridge(line // 2, low).wait_recv()
                bridge_on(line // 2, low).start()

    def arrived(line, j):
        return upright(e, line, j, m.at[line, j], m_sem.at[line, j], (r, c))

    def first(line):
        for g in range(2):
            v = convolve(lambda u, w: xpad[line + u, pl.ds(32 * g + w, 32)], 512, k1) + b1[...]
            v = jnp.where(v > 0, v, jnp.exp(jnp.minimum(v, 0.0)) - 1.0)
            e[line, pl.ds(32 * g, 32)] = v.astype(BF16).reshape(32, 16, 128)

        @pl.when(near)
        def _():
            to_corner(line).start()

        @pl.when(far)
        def _():
            to_mirror(line).start()

        @pl.when(diag)
        def _():
            spread(line, e)

    def symmetrize(line):
        for j in range(4):
            @pl.when(jnp.logical_not(stays(j)))
            def _():
                arrived(line, j).wait_recv()

        for j in range(4):
            moved = jnp.dot(p_swap[...], m[line, j].reshape(256, 128), preferred_element_type=F32)
            own = e[:, 16 * j + line].reshape(256, 128).astype(F32)
            spad[pl.ds(1, 16), line + 1, j] = (0.5 * own + moved).astype(BF16).reshape(16, 16, 128)
        each((0, 1), lambda n: s_row(n, line).start())

    def rows_in(line):
        each((0, 1), lambda n: s_row(opposite(n), line).wait_recv())

    def finish(tap, center, rows):
        v = convolve(tap, rows, k2) + b2[...]
        return (v + center.reshape(rows, 128).astype(F32)).astype(BF16)

    def second(line):
        for g in range(2):
            top = 7 * g + 1
            v = finish(lambda u, w: spad[pl.ds(top + u, 7), line + w], spad[pl.ds(top + 1, 7), line + 1], 448)
            v = v.reshape(7, 4, 16, 128)
            for j in range(4):
                xpad[pl.ds(top, 7), 16 * j + line] = v[:, j]

    def second_edge(row):
        for g in range(2):
            v = finish(lambda u, w: spad[row + u, pl.ds(8 * g + w, 8)], spad[row + 1, pl.ds(8 * g + 1, 8)], 512)
            v = v.reshape(8, 4, 16, 128)
            for j in range(4):
                xpad[row, pl.ds(16 * j + 8 * g, 8)] = v[:, j]

    def natural(part, g):
        for j in range(4):
            tiles = [xpad[pl.ds(4 * g, 4), 16 * j + 4 * part + n] for n in range(4)]
            flat[pl.ds(16 * g, 16), pl.ds(64 * j + 16 * part, 16)] = regroup(tiles)

    def at(step):
        return (step + 1) % LINES

    def zone(at_z, at_core):
        return (8 * y + 2 * (at_z // 2) + at_core, 2 * x + at_z % 2)

    up, down = (x + 1) % 4, (x + 3) % 4
    single = jnp.where(z == 3, 0, jnp.where(z == 6, 1, jnp.where(z == 0, 3, 6)))
    double = jnp.where(z == 3, 1, jnp.where(z == 6, 0, jnp.where(z == 0, 6, 3)))
    peers = [(there(*side), (r + side[0], c + side[1])) for side in SIDES]
    peers += [(far, chip(y, x)), (near, chip(x, x)), (near, chip(y, y))]
    peers += [(diag, chip(*to)) for to in ((x, up), (x, down), (up, x), (down, x))]
    peers += [(jnp.logical_not(stays(k)), (8 * y + 4 * z0 + k, 2 * x + z2)) for k in range(4)]
    peers += [(detour | bridging, zone(*to)) for to in ((single, core), (double, 0), (double, 1))]
    barrier = pltpu.get_barrier_semaphore()
    for cond, device in peers:
        @pl.when(cond)
        def _():
            pl.semaphore_signal(barrier, inc=1, device_id=device, device_id_type=MESH)

    for s in range(4):
        load(s).start()
    p_swap[...] = select(swap_phase, 0.5)
    for cond, line in ((r == 0, 0), (r == 31, 17)):
        @pl.when(cond)
        def _():
            xpad[line] = jnp.zeros((66, 16, 128), BF16)
            spad[line] = jnp.zeros((18, 4, 16, 128), BF16)
    for cond, line, group, j in ((c == 0, 0, 0, 0), (c == 7, 65, 17, 3)):
        @pl.when(cond)
        def _():
            xpad[:, line] = jnp.zeros((18, 16, 128), BF16)
            spad[:, group, j] = jnp.zeros((18, 16, 128), BF16)

    def enter(line, groups):
        for g in groups:
            rows = [flat[4 * line + n, pl.ds(64 * g, 64)].reshape(4, 16, 128) for n in range(4)]
            xpad[line + 1, pl.ds(1 + 16 * g, 16)] = regroup(rows)

    for s in range(4):
        load(s).wait()

        @pl.loop(4 * s, 4 * s + 4)
        def _(line):
            enter(line, (0, 3))

    pl.semaphore_wait(barrier, sum(cond.astype(jnp.int32) for cond, _ in peers))
    each((2, 3), lambda n: x_edge(n).start())

    @pl.loop(0, LINES)
    def _(line):
        enter(line, (1, 2))

    each((0, 1, 4, 5, 6, 7), lambda n: x_edge(n).start())
    each((2, 3), lambda n: x_edge(opposite(n)).wait_recv())

    @pl.loop(0, SYM + LINES)
    def _(t):
        @pl.when((t >= ROUTE) & (t < ROUTE + LINES))
        def _():
            route(at(t - ROUTE))

        @pl.when((t >= ROUTE + LAG) & (t < ROUTE + LAG + LINES))
        def _():
            cross_over(at(t - ROUTE - LAG))

        @pl.when(t < LINES)
        def _():
            @pl.when(t == LINES - 2)
            def _():
                each((0, 1, 4, 5, 6, 7), lambda n: x_edge(opposite(n)).wait_recv())
                each(range(8), lambda n: x_edge(n).wait_send())

            first(at(t))

        @pl.when(t >= SYM)
        def _():
            symmetrize(at(t - SYM))

        @pl.when(t == SYM + LINES - 2)
        def _():
            each((3, 5, 7), lambda n: s_edge(n).start())

        @pl.when(t == SYM + LINES - 1)
        def _():
            each((2, 4, 6), lambda n: s_edge(n).start())

        @pl.when(t > SYM + 2)
        def _():
            second(at(t - SYM - 2))

        @pl.when((t == SYM + 9) | (t == SYM + 13))
        def _():
            for g in (1, 2):
                natural((t - SYM - 5) // 4, g)

    each((2, 3, 4, 5, 6, 7), lambda n: s_edge(opposite(n)).wait_recv())
    spad[pl.ds(1, 16), 0, pl.ds(1, 3)] = spad[pl.ds(1, 16), 16, pl.ds(0, 3)]
    spad[pl.ds(1, 16), 17, pl.ds(0, 3)] = spad[pl.ds(1, 16), 1, pl.ds(1, 3)]
    for line in (15, 0, 1):
        second(line)
    for g in (1, 2):
        for part in (0, 3):
            natural(part, g)
        save(g).start()

    @pl.loop(0, LINES)
    def _(line):
        rows_in(line)

    for row in (0, 15):
        spad[row + (row > 0) * 2, 0, pl.ds(1, 3)] = spad[row + (row > 0) * 2, 16, pl.ds(0, 3)]
        spad[row + (row > 0) * 2, 17, pl.ds(0, 3)] = spad[row + (row > 0) * 2, 1, pl.ds(1, 3)]
        second_edge(row)
        for part in range(4):
            natural(part, row // 5)
        save(row // 5).start()
    each(range(2, 8), lambda n: s_edge(n).wait_send())

    @pl.loop(0, LINES)
    def _(line):
        each((0, 1), lambda n: s_row(n, line).wait_send())
        for k in range(4):
            @pl.when(jnp.logical_not(stays(k)))
            def _():
                arrived(line, k).wait_send()

        @pl.when(diag)
        def _():
            for n in range(2):
                pass_on(line, n).wait_send()

        @pl.when(jnp.logical_not(diag))
        def _():
            to_mirror(line).wait_send()

        @pl.when(bridging & (line % 2 == 1))
        def _():
            for low in range(2):
                bridge_on(line // 2, low).wait_send()

    for g in range(4):
        save(g).wait()


def body(activation, kernel_one, bias_one, kernel_two, bias_two):
    vmem, hbm = pl.BlockSpec(memory_space=pltpu.VMEM), pl.BlockSpec(memory_space=pl.ANY)
    dma = pltpu.SemaphoreType.DMA
    return pl.pallas_call(
        kernel,
        out_shape=jax.ShapeDtypeStruct(activation.shape, BF16),
        in_specs=[hbm, vmem, vmem, vmem, vmem],
        out_specs=hbm,
        scratch_shapes=[
            pltpu.VMEM((64, 256, 128), BF16),
            pltpu.VMEM((18, 66, 16, 128), BF16),
            pltpu.VMEM((16, 64, 16, 128), BF16),
            pltpu.VMEM((16, 4, 16, 16, 128), BF16),
            pltpu.VMEM((16, 64, 16, 128), BF16),
            pltpu.VMEM((2, 16, 64, 16, 128), BF16),
            pltpu.VMEM((8, 2, 16, 16, 128), BF16),
            pltpu.VMEM((18, 18, 4, 16, 128), BF16),
            pltpu.VMEM((256, 256), BF16),
            dma((4,)),
            dma((4,)),
            dma((2, 8)),
            dma((2, 8)),
            dma((2, 16)),
            dma((2, 16)),
            dma((16,)),
            dma((16,)),
            dma((2, 16)),
            dma((2, 16)),
            dma((16, 4)),
            dma((16, 4)),
            dma((8, 2)),
            dma((8, 2)),
        ],
        compiler_params=pltpu.CompilerParams(collective_id=0, has_side_effects=True, vmem_limit_bytes=60 << 20),
        name="resblock",
    )(
        activation,
        kernel_one.reshape(1152, 128),
        bias_one.reshape(1, 128),
        kernel_two.reshape(1152, 128),
        bias_two.reshape(1, 128),
    )


def solution(mesh):
    in_specs = (P("row", "col", None), P(), P(), P(), P())
    out_specs = P("row", "col", None)
    return jax.shard_map(body, mesh=mesh, in_specs=in_specs, out_specs=out_specs, check_vma=False)
```
